32 devices in a mesh: sub: 8 (over z, y), col: 4 (over x, core).
Axes of the slice: x: 2, y: 2, z: 4, core: 2. Of those that a mesh axis runs over, the one named last changes fastest.
Arguments:
- rhs: bfloat16 [32, 1024, 128], P(('sub', 'col')), may hold values from -64 to 64
- schur: bfloat16 [32, 1024, 1024], P(('sub', 'col')), may hold values from -1 to 3
- local_inverse: bfloat16 [32, 1024, 1024], P(('sub', 'col')), may hold values from -1 to 2
- basis: bfloat16 [32, 8, 1024], P(('sub', 'col')), may hold values from -0.75 to 0.75
- coarse_inverse: bfloat16 [256, 256], P('sub', 'col'), may hold values from -1 to 2
- primal_index: int32 [32, 8], P(('sub', 'col')), may hold values from 0 to 255, as said below
- neighbour_dof: int32 [32, 1024], P(('sub', 'col')), may hold values from 0 to 1023, as said below
Outputs:
- solution: bfloat16 [32, 1024, 128], P(('sub', 'col'))
The draws below stay inside these ranges and needn't reach their ends.
Inputs may be any that keep to these rules, and one draw needn't show every extreme that they name: `neighbour_dof`: each subdomain's unknowns in one shared block name places in the neighbour's facing block (for [0, 256) the neighbour's [256, 512), and so on), and the neighbour's entry names the place back. `primal_index`: every coarse unknown is named exactly once over all subdomains.
All inputs are finite; a program needn't handle non-finite values.
Results may differ from the reference program's by a relative error of at most 0.004.
The reference program's roundings to bfloat16 on the way (of `half`, `weighted`, `coarse_load`, `coarse_vector` and `coarse_solution`) count: a program that leaves them out, or rounds other values in their place, can miss the bound.
Values may be sent and summed in bfloat16 or wider, within the bound.
A program may use at most 64 MiB of HBM per device.

```python
import math
import jax
import jax.numpy as jnp
from jax import lax

IFACE = 1024
PRIM = 8
CASES = 128
SUBROWS = 8
SUBCOLS = 4
SUBS = 32
COARSE = 256


def dominant(item_key, order, lowest, highest, spread):
    diag_key, rest_key = jax.random.split(item_key)
    diag_values = jax.random.uniform(diag_key, (order,), jnp.float32, lowest, highest)
    rest = jax.random.normal(rest_key, (order, order), jnp.float32) * (spread / math.sqrt(order))
    return jnp.clip(rest + jnp.diag(diag_values), -1.0, highest)


def draw_rhs(key, part):
    base_key = jax.random.fold_in(key, 0)
    case_key = jax.random.fold_in(key, 2)
    position = jnp.arange(SUBS, dtype=jnp.float32) / max(SUBS - 1, 1)
    values = jax.random.normal(base_key, (SUBS, IFACE, CASES), jnp.float32)
    rising = jnp.exp(jnp.log(3.0) * position)
    case_scale = jnp.exp(jax.random.uniform(case_key, (CASES,), jnp.float32, 0.0, math.log(10.0)))
    return (values * rising[:, None, None] * case_scale / 5.0).astype(jnp.bfloat16)


def draw_schur(key, part):
    keys = jax.random.split(key, SUBS)
    return lax.map(lambda item_key: dominant(item_key, IFACE, 1.5, 3.0, 0.5).astype(jnp.bfloat16), keys)


def draw_local_inverse(key, part):
    keys = jax.random.split(jax.random.fold_in(key, 7), SUBS)
    return lax.map(lambda item_key: dominant(item_key, IFACE, 1.0, 2.0, 0.35).astype(jnp.bfloat16), keys)


def draw_coarse_inverse(key, part):
    return dominant(jax.random.fold_in(key, 11), COARSE, 1.0, 2.0, 0.35).astype(jnp.bfloat16)


def draw_primal_index(key, part):
    return jax.random.permutation(jax.random.fold_in(key, 13), COARSE).reshape(SUBS, PRIM).astype(jnp.int32)


def draw_neighbour_dof(key, part):
    face_size = IFACE // 4
    row_key, side_key = jax.random.split(jax.random.fold_in(key, 17))

    def orders(item_key):
        keys = jax.random.split(item_key, SUBS)
        table = jax.vmap(lambda single_key: jax.random.permutation(single_key, face_size))(keys)
        return table.reshape(SUBROWS, SUBCOLS, face_size)

    def invert(table):
        return jnp.argsort(table, axis=-1, stable=True)
    down_order = orders(row_key)
    side_order = orders(side_key)
    lower_sub = jnp.roll(invert(down_order), 1, axis=0) + face_size
    upper_sub = down_order + 0
    lower_col = jnp.roll(invert(side_order), 1, axis=1) + 3 * face_size
    upper_col = side_order + 2 * face_size
    joined = jnp.concatenate([lower_sub, upper_sub, lower_col, upper_col], axis=-1)
    return joined.reshape(SUBS, IFACE).astype(jnp.int32)


def block_scale(key, dims, shards, least, largest):
    loudness, own = 1.0, jax.random.fold_in(key, 6)
    for dim, blocks in shards:
        heights = jnp.exp(jax.random.uniform(jax.random.fold_in(own, dim), (blocks,), jnp.float32, least / len(shards), largest / len(shards)))
        loudness = loudness * jnp.repeat(heights, dims[dim] // blocks).reshape([-1 if axis == dim else 1 for axis in range(len(dims))])
    return loudness


def centred(key, extent, scale, reach, cuts=(), kind=jnp.bfloat16):
    array = jax.random.normal(key, extent, jnp.float32) * scale
    if len(cuts) > 0:
        array = block_scale(key, extent, cuts, -0.22, 0.18) * array
    return jnp.clip(array, min=-reach, max=reach).astype(kind)


def setup_inputs(seed: int = 0) -> dict:
    seeds = jax.random.split(jax.random.key(seed), 8)
    return {
        "rhs": draw_rhs(jax.random.fold_in(seeds[7], 71), 0),
        "schur": draw_schur(jax.random.fold_in(seeds[7], 71), 0),
        "local_inverse": draw_local_inverse(jax.random.fold_in(seeds[7], 71), 0),
        "basis": centred(seeds[3], (SUBS, PRIM, IFACE), (IFACE // 16) ** -0.5, 0.75, ((0, 32),)),
        "coarse_inverse": draw_coarse_inverse(jax.random.fold_in(seeds[7], 71), 0),
        "primal_index": draw_primal_index(jax.random.fold_in(seeds[7], 71), 0),
        "neighbour_dof": draw_neighbour_dof(jax.random.fold_in(seeds[7], 71), 0),
    }


def half(value):
    return value.astype(jnp.bfloat16)


def assemble(field, neighbour_dof):
    face_size = IFACE // 4
    grid_view = field.reshape(SUBROWS, SUBCOLS, IFACE, CASES)
    link_table = neighbour_dof.reshape(SUBROWS, SUBCOLS, IFACE)
    incoming = [
        jnp.roll(grid_view[:, :, face_size:2 * face_size], 1, axis=0),
        jnp.roll(grid_view[:, :, 0:face_size], -1, axis=0),
        jnp.roll(grid_view[:, :, 3 * face_size:], 1, axis=1),
        jnp.roll(grid_view[:, :, 2 * face_size:3 * face_size], -1, axis=1),
    ]
    offsets = [face_size, 0, 3 * face_size, 2 * face_size]
    picker = jax.vmap(jax.vmap(lambda source, places: source[places]))
    collected = []
    for number in range(4):
        places = link_table[:, :, number * face_size:(number + 1) * face_size] - offsets[number]
        collected.append(picker(incoming[number], places.astype(jnp.int32)))
    return field + jnp.concatenate(collected, axis=2).reshape(SUBS, IFACE, CASES)


def inner(left_field, right_field):
    return 0.5 * jnp.sum(left_field * right_field, axis=(0, 1))


def block_products(matrices, operands):
    def single(paired):
        return jnp.dot(paired[0], paired[1], preferred_element_type=jnp.float32)
    return lax.map(single, (matrices, operands))


def schur_image(direction, schur, neighbour_dof):
    return assemble(block_products(schur, half(direction)), neighbour_dof)


def precondition(residual, local_inverse, basis, coarse_inverse, primal_index, neighbour_dof):
    weighted = half(residual * 0.5)
    local_part = block_products(local_inverse, weighted)
    coarse_load = half(block_products(basis, weighted))
    coarse_vector = jnp.zeros((COARSE, CASES), jnp.bfloat16)
    coarse_vector = coarse_vector.at[primal_index.reshape(-1)].set(coarse_load.reshape(SUBS * PRIM, CASES))
    coarse_solution = half(jnp.dot(coarse_inverse, coarse_vector, preferred_element_type=jnp.float32))
    taken = coarse_solution[primal_index]

    def lift(paired):
        return lax.dot_general(paired[0], paired[1], (((0,), (0,)), ((), ())), preferred_element_type=jnp.float32)

    correction = lax.map(lift, (basis, taken))
    return assemble((local_part + correction) * 0.5, neighbour_dof)


def reference(rhs, schur, local_inverse, basis, coarse_inverse, primal_index, neighbour_dof):
    residual = assemble(rhs.astype(jnp.float32), neighbour_dof)
    first = precondition(residual, local_inverse, basis, coarse_inverse, primal_index, neighbour_dof)
    rz_first = inner(residual, first)
    image = schur_image(first, schur, neighbour_dof)
    alpha = rz_first / inner(first, image)
    return half(alpha * first)
```

```python
import functools
import math

import jax
import jax.numpy as jnp
from jax import lax
from jax.experimental import pallas as pl
from jax.experimental.pallas import tpu as pltpu
from jax.sharding import PartitionSpec as P

MESH = pl.DeviceIdType.MESH
F32 = jnp.float32
BF16 = jnp.bfloat16


def kernel(
    subs, cols,
    rhs_hbm, schur_hbm, inverse_hbm, basis_ref, coarse_ref, index_ref, links_ref,
    out_ref,
    rhs_ref, schur_ref, inverse_ref, picks, halo_rhs, halo_z, weighted, z_ref, z_half, first_ref, p_half,
    indices, chosen, arrived, columns, rows_ref, loads, sums,
    local_sem, halo_send, halo_recv, z_send, z_recv, all_send, all_recv,
):
    count = subs * cols
    row = lax.axis_index("sub")
    column = lax.axis_index("col")
    me = row * cols + column
    size = rhs_ref.shape[0]
    face = size // 4
    primals = index_ref.shape[1]
    height, width = coarse_ref.shape
    group = math.gcd(count, 32)

    def place(target):
        return (target // cols, target % cols)

    neighbours = (
        ((row + subs - 1) % subs, column),
        ((row + 1) % subs, column),
        (row, (column + cols - 1) % cols),
        (row, (column + 1) % cols),
    )

    barrier = pltpu.get_barrier_semaphore()

    def greet(step, carry):
        pl.semaphore_signal(
            barrier, inc=1, device_id=place((me + step) % count), device_id_type=MESH
        )
        return carry

    lax.fori_loop(1, count, greet, 0)

    load_rhs = pltpu.make_async_copy(rhs_hbm.at[0], rhs_ref, local_sem.at[0])
    load_inverse = pltpu.make_async_copy(inverse_hbm.at[0], inverse_ref, local_sem.at[1])
    load_schur = pltpu.make_async_copy(schur_hbm.at[0], schur_ref, local_sem.at[2])
    load_rhs.start()
    load_inverse.start()
    load_schur.start()

    lanes = indices.shape[2]
    indices[me] = jnp.zeros((1, lanes), F32)
    indices[me, :, pl.ds(0, primals)] = index_ref[...].astype(F32)

    offsets = (face, 0, 3 * face, 2 * face)
    for f in range(4):
        places = links_ref[:, f * face : (f + 1) * face] - offsets[f]
        hit = lax.broadcasted_iota(jnp.int32, (face, face), 0) == places
        picks[f] = jnp.where(hit, 1.0, 0.0).astype(F32).T.astype(BF16)

    pl.semaphore_wait(barrier, count - 1)

    def halo_copies(source, target, send, recv):
        copies = []
        for g in range(4):
            copies.append(
                pltpu.make_async_remote_copy(
                    src_ref=source(g),
                    dst_ref=target.at[g ^ 1],
                    send_sem=send.at[g],
                    recv_sem=recv.at[g ^ 1],
                    device_id=neighbours[g],
                    device_id_type=MESH,
                )
            )
        return copies

    def broadcast(slots, number):
        def send(step, carry):
            pltpu.make_async_remote_copy(
                src_ref=slots.at[me],
                dst_ref=slots.at[me],
                send_sem=all_send.at[number],
                recv_sem=all_recv.at[number],
                device_id=place((me + step) % count),
                device_id_type=MESH,
            ).start()
            return carry

        lax.fori_loop(1, count, send, 0)

    def wait_all(slots, sems, number):
        part = slots.at[pl.ds(0, count - 1)]
        pltpu.make_async_copy(part, part, sems.at[number]).wait()

    rhs_copies = halo_copies(
        lambda g: rhs_hbm.at[0, pl.ds(g * face, face)], halo_rhs, halo_send, halo_recv
    )
    for copy in rhs_copies:
        copy.start()
    broadcast(indices, 0)

    basis = basis_ref[0]
    basis_t = basis.astype(F32).T.astype(BF16)
    load_rhs.wait()

    for copy in rhs_copies:
        copy.wait_recv()
    for f in range(4):
        block = pl.ds(f * face, face)
        got = jnp.dot(picks[f], halo_rhs[f], preferred_element_type=F32)
        residual = rhs_ref[block, :].astype(F32) + got
        first_ref[block, :] = residual
        weighted[block, :] = (residual * 0.5).astype(BF16)
    loads[me] = jnp.dot(basis, weighted[...], preferred_element_type=F32).astype(BF16)
    broadcast(loads, 1)

    wait_all(indices, all_recv, 0)

    def spread(g, extent):
        values = indices[pl.ds(g * group, group)]
        values = jnp.broadcast_to(values, (group, primals, lanes))
        diagonal = lax.broadcasted_iota(jnp.int32, values.shape, 1) == lax.broadcasted_iota(
            jnp.int32, values.shape, 2
        )
        named = jnp.sum(jnp.where(diagonal, values, 0.0), axis=2, keepdims=True)
        named = named.astype(jnp.int32)
        return jnp.broadcast_to(named, (group, primals, extent))

    def choose(g, carry):
        named = spread(g, height) - row * height
        hit = lax.broadcasted_iota(jnp.int32, named.shape, 2) == named
        hit = jnp.where(hit, 1.0, 0.0).astype(F32).reshape(group * primals, height).astype(BF16)
        picked = jnp.dot(hit, coarse_ref[...], preferred_element_type=F32)
        chosen[pl.ds(g * group, group)] = picked.reshape(group, primals, width).astype(BF16)
        return carry

    lax.fori_loop(0, count // group, choose, 0)
    arrived[me] = chosen[me]

    def send_rows(step, carry):
        target = (me + step) % count
        pltpu.make_async_remote_copy(
            src_ref=chosen.at[target],
            dst_ref=arrived.at[me],
            send_sem=all_send.at[2],
            recv_sem=all_recv.at[2],
            device_id=place(target),
            device_id_type=MESH,
        ).start()
        return carry

    lax.fori_loop(1, count, send_rows, 0)

    load_inverse.wait()
    for f in range(4):
        block = pl.ds(f * face, face)
        z_ref[block, :] = jnp.dot(inverse_ref[block, :], weighted[...], preferred_element_type=F32)

    wait_all(arrived, all_recv, 2)
    for j in range(cols):
        def add(i, total):
            return total + arrived[i * cols + j].astype(F32)

        rows_ref[j] = lax.fori_loop(0, subs, add, jnp.zeros((primals, width), F32), unroll=subs <= 8)

    def arrange(g, carry):
        total = jnp.zeros((primals, group * primals), F32)
        for j in range(cols):
            named = spread(g, width) - j * width
            hit = lax.broadcasted_iota(jnp.int32, named.shape, 2) == named
            hit = jnp.where(hit, 1.0, 0.0).astype(F32).reshape(group * primals, width).astype(BF16)
            total += lax.dot_general(
                rows_ref[j].astype(BF16), hit, (((1,), (1,)), ((), ())), preferred_element_type=F32
            )
        columns[g] = total
        return carry

    lax.fori_loop(0, count // group, arrange, 0)

    wait_all(loads, all_recv, 1)

    def solve(g, total):
        part = loads[pl.ds(g * group, group)].astype(F32).reshape(group * primals, loads.shape[2])
        return total + jnp.dot(columns[g].astype(BF16), part.astype(BF16), preferred_element_type=F32)

    taken = lax.fori_loop(
        0, count // group, solve, jnp.zeros((primals, loads.shape[2]), F32)
    ).astype(BF16)

    correction = jnp.dot(basis_t, taken, preferred_element_type=F32)
    z_value = (z_ref[...] + correction) * 0.5
    z_ref[...] = z_value
    z_half[...] = z_value.astype(BF16)
    z_copies = halo_copies(lambda g: z_half.at[pl.ds(g * face, face)], halo_z, z_send, z_recv)
    for copy in z_copies:
        copy.start()
    sums[me, pl.ds(0, 1), :] = jnp.sum(first_ref[...] * z_ref[...], axis=0, keepdims=True)
    load_schur.wait()
    for copy in z_copies:
        copy.wait_recv()
    for f in range(4):
        block = pl.ds(f * face, face)
        first = z_ref[block, :] + jnp.dot(picks[f], halo_z[f], preferred_element_type=F32)
        first_ref[block, :] = first
        p_half[block, :] = first.astype(BF16)
    total = jnp.zeros((1, first_ref.shape[1]), F32)
    for f in range(4):
        block = pl.ds(f * face, face)
        image = jnp.dot(schur_ref[block, :], p_half[...], preferred_element_type=F32)
        total += jnp.sum(first_ref[block, :] * image, axis=0, keepdims=True)
    sums[me, pl.ds(1, 1), :] = total
    broadcast(sums, 3)

    for copy in rhs_copies + z_copies:
        copy.wait_send()
    wait_all(indices, all_send, 0)
    wait_all(loads, all_send, 1)
    wait_all(arrived, all_send, 2)
    wait_all(sums, all_recv, 3)
    whole = jnp.sum(sums[...], axis=0)
    alpha = whole[0:1, :] / whole[1:2, :]
    out_ref[0] = (alpha * first_ref[...]).astype(BF16)
    wait_all(sums, all_send, 3)


def solution(mesh):
    subs, cols = mesh.shape["sub"], mesh.shape["col"]
    count = subs * cols

    def step(rhs, schur, local_inverse, basis, coarse_inverse, primal_index, neighbour_dof):
        size, cases = rhs.shape[1:]
        face = size // 4
        primals = primal_index.shape[1]
        height, width = coarse_inverse.shape
        lanes = 128 * pl.cdiv(primals, 128)
        group = math.gcd(count, 32)
        anywhere = pl.BlockSpec(memory_space=pl.ANY)
        near = pl.BlockSpec(memory_space=pltpu.VMEM)
        return pl.pallas_call(
            functools.partial(kernel, subs, cols),
            out_shape=jax.ShapeDtypeStruct(rhs.shape, BF16),
            in_specs=[anywhere] * 3 + [near] * 4,
            out_specs=near,
            scratch_shapes=[
                pltpu.VMEM((size, cases), BF16),
                pltpu.VMEM((size, size), BF16),
                pltpu.VMEM((size, size), BF16),
                pltpu.VMEM((4, face, face), BF16),
                pltpu.VMEM((4, face, cases), BF16),
                pltpu.VMEM((4, face, cases), BF16),
                pltpu.VMEM((size, cases), BF16),
                pltpu.VMEM((size, cases), F32),
                pltpu.VMEM((size, cases), BF16),
                pltpu.VMEM((size, cases), F32),
                pltpu.VMEM((size, cases), BF16),
                pltpu.VMEM((count, 1, lanes), F32),
                pltpu.VMEM((count, primals, width), BF16),
                pltpu.VMEM((count, primals, width), BF16),
                pltpu.VMEM((count // group, primals, group * primals), F32),
                pltpu.VMEM((cols, primals, width), F32),
                pltpu.VMEM((count, primals, cases), BF16),
                pltpu.VMEM((count, 2, cases), F32),
                pltpu.SemaphoreType.DMA((3,)),
                pltpu.SemaphoreType.DMA((4,)),
                pltpu.SemaphoreType.DMA((4,)),
                pltpu.SemaphoreType.DMA((4,)),
                pltpu.SemaphoreType.DMA((4,)),
                pltpu.SemaphoreType.DMA((4,)),
                pltpu.SemaphoreType.DMA((4,)),
            ],
            compiler_params=pltpu.CompilerParams(
                collective_id=0, has_side_effects=True, vmem_limit_bytes=60 * 1024 * 1024
            ),
        )(rhs, schur, local_inverse, basis, coarse_inverse, primal_index, neighbour_dof)

    return jax.shard_map(
        step,
        mesh=mesh,
        in_specs=(
            P(("sub", "col"), None, None),
            P(("sub", "col"), None, None),
            P(("sub", "col"), None, None),
            P(("sub", "col"), None, None),
            P("sub", "col"),
            P(("sub", "col"), None),
            P(("sub", "col"), None),
        ),
        out_specs=P(("sub", "col"), None, None),
        check_vma=False,
    )
```

```python
import functools
import math

import jax
import jax.numpy as jnp
from jax import lax
from jax.experimental import pallas as pl
from jax.experimental.pallas import tpu as pltpu
from jax.sharding import PartitionSpec as P

MESH = pl.DeviceIdType.MESH
F32 = jnp.float32
BF16 = jnp.bfloat16
UNROLL = False


def kernel(
    subs, cols,
    rhs_hbm, schur_hbm, inverse_hbm, basis_hbm, coarse_hbm, index_hbm, links_hbm,
    first_out, alpha_ref,
    basis_ref, coarse_ref, index_ref, links_ref,
    rhs_ref, schur_ref, inverse_ref, picks, halo_rhs, halo_z, weighted, z_ref, z_half, first_ref, p_half,
    image_ref, indices, chosen, arrived, vector, loads, sums,
    local_sem, halo_send, halo_recv, z_send, z_recv, all_send, all_recv,
):
    count = subs * cols
    row = lax.axis_index("sub")
    column = lax.axis_index("col")
    me = row * cols + column
    size = rhs_ref.shape[0]
    face = size // 4
    primals = index_ref.shape[1]
    height, width = coarse_ref.shape
    group = math.gcd(count, 32)

    def place(target):
        return (target // cols, target % cols)

    neighbours = (
        ((row + subs - 1) % subs, column),
        ((row + 1) % subs, column),
        (row, (column + cols - 1) % cols),
        (row, (column + 1) % cols),
    )

    half_way = (row * 2) // subs

    def each_other(act):
        def body(step, carry):
            q = step // cols
            target_row = (1 - half_way) * (subs - 1 - q) + half_way * q
            target = target_row * cols + (column + step) % cols

            @pl.when(target != me)
            def _():
                act(target)

            return carry

        lax.fori_loop(0, count, body, 0, unroll=UNROLL and count <= 64)

    barrier = pltpu.get_barrier_semaphore()

    each_other(
        lambda target: pl.semaphore_signal(
            barrier, inc=1, device_id=place(target), device_id_type=MESH
        )
    )

    small_loads = [
        pltpu.make_async_copy(source, target, local_sem.at[4 + number])
        for number, (source, target) in enumerate(
            ((links_hbm, links_ref), (index_hbm, index_ref), (basis_hbm, basis_ref), (coarse_hbm, coarse_ref))
        )
    ]
    for load in small_loads:
        load.start()
    load_rhs = pltpu.make_async_copy(rhs_hbm.at[0], rhs_ref, local_sem.at[0])
    load_inverse = pltpu.make_async_copy(inverse_hbm.at[0], inverse_ref, local_sem.at[1])
    load_schur = pltpu.make_async_copy(schur_hbm.at[0], schur_ref, local_sem.at[2])
    load_rhs.start()
    load_inverse.start()
    load_schur.start()
    for load in small_loads:
        load.wait()

    lanes = indices.shape[2]
    indices[me] = jnp.zeros((1, lanes), F32)
    indices[me, :, pl.ds(0, primals)] = index_ref[...].astype(F32)

    offsets = (face, 0, 3 * face, 2 * face)
    for f in range(4):
        places = links_ref[:, f * face : (f + 1) * face] - offsets[f]
        hit = lax.broadcasted_iota(jnp.int32, (face, face), 0) == places
        picks[f] = jnp.where(hit, 1.0, 0.0).astype(F32).T.astype(BF16)

    pl.semaphore_wait(barrier, count - 1)

    def halo_copies(source, target, send, recv):
        copies = []
        for g in range(4):
            copies.append(
                pltpu.make_async_remote_copy(
                    src_ref=source(g),
                    dst_ref=target.at[g ^ 1],
                    send_sem=send.at[g],
                    recv_sem=recv.at[g ^ 1],
                    device_id=neighbours[g],
                    device_id_type=MESH,
                )
            )
        return copies

    def broadcast(slots, number):
        each_other(
            lambda target: pltpu.make_async_remote_copy(
                src_ref=slots.at[me],
                dst_ref=slots.at[me],
                send_sem=all_send.at[number],
                recv_sem=all_recv.at[number],
                device_id=place(target),
                device_id_type=MESH,
            ).start()
        )

    def wait_all(slots, sems, number):
        part = slots.at[pl.ds(0, count - 1)]
        pltpu.make_async_copy(part, part, sems.at[number]).wait()

    rhs_copies = halo_copies(
        lambda g: rhs_hbm.at[0, pl.ds(g * face, face)], halo_rhs, halo_send, halo_recv
    )
    for copy in rhs_copies:
        copy.start()
    broadcast(indices, 0)

    basis = basis_ref[0]
    basis_t = basis.astype(F32).T.astype(BF16)
    load_rhs.wait()

    load = jnp.zeros((primals, rhs_ref.shape[1]), F32)
    for f in (2, 3, 0, 1):
        block = pl.ds(f * face, face)
        rhs_copies[f ^ 1].wait_recv()
        got = jnp.dot(picks[f], halo_rhs[f], preferred_element_type=F32)
        residual = rhs_ref[block, :].astype(F32) + got
        first_ref[block, :] = residual
        part = (residual * 0.5).astype(BF16)
        weighted[block, :] = part
        load += jnp.dot(basis[:, f * face : (f + 1) * face], part, preferred_element_type=F32)
    loads[me] = load.astype(BF16)
    broadcast(loads, 1)

    wait_all(indices, all_recv, 0)

    def spread(g, extent):
        values = indices[pl.ds(g * group, group)]
        values = jnp.broadcast_to(values, (group, primals, lanes))
        diagonal = lax.broadcasted_iota(jnp.int32, values.shape, 1) == lax.broadcasted_iota(
            jnp.int32, values.shape, 2
        )
        named = jnp.sum(jnp.where(diagonal, values, 0.0), axis=2, keepdims=True)
        named = named.astype(jnp.int32)
        return jnp.broadcast_to(named, (group, primals, extent))

    def choose(g, carry):
        named = spread(g, height) - row * height
        hit = lax.broadcasted_iota(jnp.int32, named.shape, 2) == named
        hit = jnp.where(hit, 1.0, 0.0).astype(F32).reshape(group * primals, height).astype(BF16)
        picked = jnp.dot(hit, coarse_ref[...], preferred_element_type=F32)
        chosen[pl.ds(g * group, group)] = picked.reshape(group, primals, width).astype(BF16)
        return carry

    lax.fori_loop(0, count // group, choose, 0)
    arrived[me] = chosen[me]

    each_other(
        lambda target: pltpu.make_async_remote_copy(
            src_ref=chosen.at[target],
            dst_ref=arrived.at[me],
            send_sem=all_send.at[2],
            recv_sem=all_recv.at[2],
            device_id=place(target),
            device_id_type=MESH,
        ).start()
    )

    load_inverse.wait()
    for f in range(4):
        block = pl.ds(f * face, face)
        z_ref[block, :] = jnp.dot(inverse_ref[block, :], weighted[...], preferred_element_type=F32)

    wait_all(loads, all_recv, 1)
    vector[...] = jnp.zeros_like(vector)

    def gather(g, carry):
        part = loads[pl.ds(g * group, group)].astype(F32).reshape(group * primals, loads.shape[2])
        part = part.astype(BF16)
        for j in range(cols):
            named = spread(g, width) - j * width
            hit = lax.broadcasted_iota(jnp.int32, named.shape, 2) == named
            hit = jnp.where(hit, 1.0, 0.0).astype(F32).reshape(group * primals, width).astype(BF16)
            vector[j] += lax.dot_general(
                hit, part, (((0,), (0,)), ((), ())), preferred_element_type=F32
            )
        return carry

    lax.fori_loop(0, count // group, gather, 0)

    wait_all(arrived, all_recv, 2)
    taken = jnp.zeros((primals, loads.shape[2]), F32)
    for j in range(cols):
        def add(i, total):
            return total + arrived[i * cols + j].astype(F32)

        rows = lax.fori_loop(0, subs, add, jnp.zeros((primals, width), F32), unroll=subs <= 8)
        taken += jnp.dot(rows.astype(BF16), vector[j].astype(BF16), preferred_element_type=F32)
    taken = taken.astype(BF16)

    z_copies = halo_copies(lambda g: z_half.at[pl.ds(g * face, face)], halo_z, z_send, z_recv)
    for f in range(4):
        block = pl.ds(f * face, face)
        correction = jnp.dot(
            basis_t[f * face : (f + 1) * face, :], taken, preferred_element_type=F32
        )
        z_value = (z_ref[block, :] + correction) * 0.5
        z_ref[block, :] = z_value
        z_half[block, :] = z_value.astype(BF16)
        z_copies[f].start()
    sums[me, pl.ds(0, 1), :] = jnp.sum(first_ref[...] * z_ref[...], axis=0, keepdims=True)
    load_schur.wait()
    for pair in ((2, 3), (0, 1)):
        for f in pair:
            block = pl.ds(f * face, face)
            z_copies[f ^ 1].wait_recv()
            first = z_ref[block, :] + jnp.dot(picks[f], halo_z[f], preferred_element_type=F32)
            first_ref[block, :] = first
            p_half[block, :] = first.astype(BF16)
        both = pl.ds(pair[0] * face, 2 * face)
        if pair[0] == 2:
            for f in range(4):
                block = pl.ds(f * face, face)
                image_ref[block, :] = jnp.dot(
                    schur_ref[block, both], p_half[both, :], preferred_element_type=F32
                )
    total = jnp.zeros((1, first_ref.shape[1]), F32)
    for f in range(4):
        block = pl.ds(f * face, face)
        image = image_ref[block, :] + jnp.dot(
            schur_ref[block, both], p_half[both, :], preferred_element_type=F32
        )
        total += jnp.sum(first_ref[block, :] * image, axis=0, keepdims=True)
    sums[me, pl.ds(1, 1), :] = total
    broadcast(sums, 3)
    store = pltpu.make_async_copy(first_ref, first_out, local_sem.at[3])
    store.start()

    for copy in rhs_copies + z_copies:
        copy.wait_send()
    wait_all(indices, all_send, 0)
    wait_all(loads, all_send, 1)
    wait_all(arrived, all_send, 2)
    wait_all(sums, all_recv, 3)
    whole = jnp.sum(sums[...], axis=0)
    alpha_ref[...] = whole[0:1, :] / whole[1:2, :]
    store.wait()
    wait_all(sums, all_send, 3)


def solution(mesh):
    subs, cols = mesh.shape["sub"], mesh.shape["col"]
    count = subs * cols

    def step(rhs, schur, local_inverse, basis, coarse_inverse, primal_index, neighbour_dof):
        size, cases = rhs.shape[1:]
        face = size // 4
        primals = primal_index.shape[1]
        height, width = coarse_inverse.shape
        lanes = 128 * pl.cdiv(primals, 128)
        anywhere = pl.BlockSpec(memory_space=pl.ANY)
        near = pl.BlockSpec(memory_space=pltpu.VMEM)
        first, alpha = pl.pallas_call(
            functools.partial(kernel, subs, cols),
            out_shape=(
                jax.ShapeDtypeStruct((size, cases), F32),
                jax.ShapeDtypeStruct((1, cases), F32),
            ),
            in_specs=[anywhere] * 7,
            out_specs=(anywhere, near),
            scratch_shapes=[
                pltpu.VMEM(basis.shape, BF16),
                pltpu.VMEM(coarse_inverse.shape, BF16),
                pltpu.VMEM(primal_index.shape, jnp.int32),
                pltpu.VMEM(neighbour_dof.shape, jnp.int32),
                pltpu.VMEM((size, cases), BF16),
                pltpu.VMEM((size, size), BF16),
                pltpu.VMEM((size, size), BF16),
                pltpu.VMEM((4, face, face), BF16),
                pltpu.VMEM((4, face, cases), BF16),
                pltpu.VMEM((4, face, cases), BF16),
                pltpu.VMEM((size, cases), BF16),
                pltpu.VMEM((size, cases), F32),
                pltpu.VMEM((size, cases), BF16),
                pltpu.VMEM((size, cases), F32),
                pltpu.VMEM((size, cases), BF16),
                pltpu.VMEM((size, cases), F32),
                pltpu.VMEM((count, 1, lanes), F32),
                pltpu.VMEM((count, primals, width), BF16),
                pltpu.VMEM((count, primals, width), BF16),
                pltpu.VMEM((cols, width, cases), F32),
                pltpu.VMEM((count, primals, cases), BF16),
                pltpu.VMEM((count, 2, cases), F32),
                pltpu.SemaphoreType.DMA((8,)),
                pltpu.SemaphoreType.DMA((4,)),
                pltpu.SemaphoreType.DMA((4,)),
                pltpu.SemaphoreType.DMA((4,)),
                pltpu.SemaphoreType.DMA((4,)),
                pltpu.SemaphoreType.DMA((4,)),
                pltpu.SemaphoreType.DMA((4,)),
            ],
            compiler_params=pltpu.CompilerParams(
                collective_id=0, has_side_effects=True, vmem_limit_bytes=60 * 1024 * 1024
            ),
        )(rhs, schur, local_inverse, basis, coarse_inverse, primal_index, neighbour_dof)
        return (alpha * first).astype(BF16)[None]

    return jax.shard_map(
        step,
        mesh=mesh,
        in_specs=(
            P(("sub", "col"), None, None),
            P(("sub", "col"), None, None),
            P(("sub", "col"), None, None),
            P(("sub", "col"), None, None),
            P("sub", "col"),
            P(("sub", "col"), None),
            P(("sub", "col"), None),
        ),
        out_specs=P(("sub", "col"), None, None),
        check_vma=False,
    )
```

```python
import functools
import math

import jax
import jax.numpy as jnp
from jax import lax
from jax.experimental import pallas as pl
from jax.experimental.pallas import tpu as pltpu
from jax.sharding import PartitionSpec as P

MESH = pl.DeviceIdType.MESH
F32 = jnp.float32
BF16 = jnp.bfloat16
UNROLL = True


def kernel(
    subs, cols,
    rhs_hbm, schur_hbm, inverse_hbm, basis_hbm, coarse_hbm, index_hbm, links_hbm,
    first_ref, alpha_ref,
    basis_ref, coarse_ref, index_ref, links_ref,
    rhs_ref, schur_ref, inverse_ref, picks, halo_rhs, halo_z, weighted, z_ref, z_half, p_half,
    image_ref, indices, chosen, arrived, vector, loads, sums,
    local_sem, halo_send, halo_recv, z_send, z_recv, all_send, all_recv,
):
    count = subs * cols
    row = lax.axis_index("sub")
    column = lax.axis_index("col")
    me = row * cols + column
    size = rhs_ref.shape[0]
    face = size // 4
    primals = index_ref.shape[1]
    height, width = coarse_ref.shape
    group = math.gcd(count, 32)

    def place(target):
        return (target // cols, target % cols)

    half_way = (row * 2) // subs

    def each_other(act):
        def body(step, carry):
            q = step // cols
            target_row = (1 - half_way) * (subs - 1 - q) + half_way * q
            target = target_row * cols + (column + step) % cols

            @pl.when(target != me)
            def _():
                act(target)

            return carry

        lax.fori_loop(0, count, body, 0, unroll=UNROLL and count <= 64)

    barrier = pltpu.get_barrier_semaphore()

    each_other(
        lambda target: pl.semaphore_signal(
            barrier, inc=1, device_id=place(target), device_id_type=MESH
        )
    )

    small_loads = [
        pltpu.make_async_copy(source, target, local_sem.at[4 + number])
        for number, (source, target) in enumerate(
            ((links_hbm, links_ref), (index_hbm, index_ref), (basis_hbm, basis_ref), (coarse_hbm, coarse_ref))
        )
    ]
    for load in small_loads:
        load.start()
    load_rhs = pltpu.make_async_copy(rhs_hbm.at[0], rhs_ref, local_sem.at[0])
    load_inverse = pltpu.make_async_copy(inverse_hbm.at[0], inverse_ref, local_sem.at[1])
    load_schur = pltpu.make_async_copy(schur_hbm.at[0], schur_ref, local_sem.at[2])
    load_rhs.start()
    load_inverse.start()
    load_schur.start()
    for load in small_loads:
        load.wait()

    lanes = indices.shape[2]
    indices[me] = jnp.zeros((1, lanes), F32)
    indices[me, :, pl.ds(0, primals)] = index_ref[...].astype(F32)

    offsets = (face, 0, 3 * face, 2 * face)
    for f in range(4):
        places = links_ref[:, f * face : (f + 1) * face] - offsets[f]
        hit = lax.broadcasted_iota(jnp.int32, (face, face), 0) == places
        picks[f] = jnp.where(hit, 1.0, 0.0).astype(F32).T.astype(BF16)

    pl.semaphore_wait(barrier, count - 1)

    swap = row % 2

    def halo_copies(source, target, send, recv):
        copies = []
        for g in (swap, 1 - swap, 2, 3):
            if isinstance(g, int):
                facing = 5 - g
                partner = (row, (column + cols + 2 * g - 5) % cols)
            else:
                facing = 1 - g
                partner = ((row + subs + 2 * g - 1) % subs, column)
            copies.append(
                pltpu.make_async_remote_copy(
                    src_ref=source(g),
                    dst_ref=target.at[facing],
                    send_sem=send.at[g],
                    recv_sem=recv.at[facing],
                    device_id=partner,
                    device_id_type=MESH,
                )
            )
        return copies

    def wait_face(target, recv, f):
        pltpu.make_async_copy(target.at[f], target.at[f], recv.at[f]).wait()

    def broadcast(slots, number):
        each_other(
            lambda target: pltpu.make_async_remote_copy(
                src_ref=slots.at[me],
                dst_ref=slots.at[me],
                send_sem=all_send.at[number],
                recv_sem=all_recv.at[number],
                device_id=place(target),
                device_id_type=MESH,
            ).start()
        )

    def wait_all(slots, sems, number):
        part = slots.at[pl.ds(0, count - 1)]
        pltpu.make_async_copy(part, part, sems.at[number]).wait()

    rhs_copies = halo_copies(
        lambda g: rhs_hbm.at[0, pl.ds(g * face, face)], halo_rhs, halo_send, halo_recv
    )
    for copy in rhs_copies:
        copy.start()
    broadcast(indices, 0)

    basis = basis_ref[0]
    basis_t = basis.astype(F32).T.astype(BF16)
    load_rhs.wait()

    load = jnp.zeros((primals, rhs_ref.shape[1]), F32)
    for f in (2, 3, 0, 1):
        block = pl.ds(f * face, face)
        wait_face(halo_rhs, halo_recv, f)
        got = jnp.dot(picks[f], halo_rhs[f], preferred_element_type=F32)
        residual = rhs_ref[block, :].astype(F32) + got
        first_ref[block, :] = residual
        part = (residual * 0.5).astype(BF16)
        weighted[block, :] = part
        load += jnp.dot(basis[:, f * face : (f + 1) * face], part, preferred_element_type=F32)
    loads[me] = load.astype(BF16)
    broadcast(loads, 1)

    wait_all(indices, all_recv, 0)

    def spread(g, extent):
        values = indices[pl.ds(g * group, group)]
        values = jnp.broadcast_to(values, (group, primals, lanes))
        diagonal = lax.broadcasted_iota(jnp.int32, values.shape, 1) == lax.broadcasted_iota(
            jnp.int32, values.shape, 2
        )
        named = jnp.sum(jnp.where(diagonal, values, 0.0), axis=2, keepdims=True)
        named = named.astype(jnp.int32)
        return jnp.broadcast_to(named, (group, primals, extent))

    def choose(g, carry):
        named = spread(g, height) - row * height
        hit = lax.broadcasted_iota(jnp.int32, named.shape, 2) == named
        hit = jnp.where(hit, 1.0, 0.0).astype(F32).reshape(group * primals, height).astype(BF16)
        picked = jnp.dot(hit, coarse_ref[...], preferred_element_type=F32)
        chosen[pl.ds(g * group, group)] = picked.reshape(group, primals, width).astype(BF16)
        return carry

    lax.fori_loop(0, count // group, choose, 0)
    arrived[me] = chosen[me]

    each_other(
        lambda target: pltpu.make_async_remote_copy(
            src_ref=chosen.at[target],
            dst_ref=arrived.at[me],
            send_sem=all_send.at[2],
            recv_sem=all_recv.at[2],
            device_id=place(target),
            device_id_type=MESH,
        ).start()
    )

    load_inverse.wait()
    for f in range(4):
        block = pl.ds(f * face, face)
        z_ref[block, :] = jnp.dot(inverse_ref[block, :], weighted[...], preferred_element_type=F32)

    wait_all(loads, all_recv, 1)
    vector[...] = jnp.zeros_like(vector)

    def gather(g, carry):
        part = loads[pl.ds(g * group, group)].astype(F32).reshape(group * primals, loads.shape[2])
        part = part.astype(BF16)
        for j in range(cols):
            named = spread(g, width) - j * width
            hit = lax.broadcasted_iota(jnp.int32, named.shape, 2) == named
            hit = jnp.where(hit, 1.0, 0.0).astype(F32).reshape(group * primals, width).astype(BF16)
            vector[j] += lax.dot_general(
                hit, part, (((0,), (0,)), ((), ())), preferred_element_type=F32
            )
        return carry

    lax.fori_loop(0, count // group, gather, 0)

    wait_all(arrived, all_recv, 2)
    taken = jnp.zeros((primals, loads.shape[2]), F32)
    for j in range(cols):
        def add(i, total):
            return total + arrived[i * cols + j].astype(F32)

        rows = lax.fori_loop(0, subs, add, jnp.zeros((primals, width), F32), unroll=subs <= 8)
        taken += jnp.dot(rows.astype(BF16), vector[j].astype(BF16), preferred_element_type=F32)
    taken = taken.astype(BF16)

    z_copies = halo_copies(lambda g: z_half.at[pl.ds(g * face, face)], halo_z, z_send, z_recv)
    for f in range(4):
        block = pl.ds(f * face, face)
        correction = jnp.dot(
            basis_t[f * face : (f + 1) * face, :], taken, preferred_element_type=F32
        )
        z_value = (z_ref[block, :] + correction) * 0.5
        z_ref[block, :] = z_value
        z_half[block, :] = z_value.astype(BF16)
        if f == 1:
            z_copies[0].start()
            z_copies[1].start()
        if f > 1:
            z_copies[f].start()
    sums[me, pl.ds(0, 1), :] = jnp.sum(first_ref[...] * z_ref[...], axis=0, keepdims=True)
    load_schur.wait()
    for pair in ((2, 3), (0, 1)):
        for f in pair:
            block = pl.ds(f * face, face)
            wait_face(halo_z, z_recv, f)
            first = z_ref[block, :] + jnp.dot(picks[f], halo_z[f], preferred_element_type=F32)
            first_ref[block, :] = first
            p_half[block, :] = first.astype(BF16)
        both = pl.ds(pair[0] * face, 2 * face)
        if pair[0] == 2:
            for f in range(4):
                block = pl.ds(f * face, face)
                image_ref[block, :] = jnp.dot(
                    schur_ref[block, both], p_half[both, :], preferred_element_type=F32
                )
    total = jnp.zeros((1, first_ref.shape[1]), F32)
    for f in range(4):
        block = pl.ds(f * face, face)
        image = image_ref[block, :] + jnp.dot(
            schur_ref[block, both], p_half[both, :], preferred_element_type=F32
        )
        total += jnp.sum(first_ref[block, :] * image, axis=0, keepdims=True)
    sums[me, pl.ds(1, 1), :] = total
    broadcast(sums, 3)
    for copy in rhs_copies + z_copies:
        copy.wait_send()
    wait_all(indices, all_send, 0)
    wait_all(loads, all_send, 1)
    wait_all(arrived, all_send, 2)
    wait_all(sums, all_recv, 3)
    whole = jnp.sum(sums[...], axis=0)
    alpha_ref[...] = whole[0:1, :] / whole[1:2, :]
    wait_all(sums, all_send, 3)


def solution(mesh):
    subs, cols = mesh.shape["sub"], mesh.shape["col"]
    count = subs * cols

    def step(rhs, schur, local_inverse, basis, coarse_inverse, primal_index, neighbour_dof):
        size, cases = rhs.shape[1:]
        face = size // 4
        primals = primal_index.shape[1]
        height, width = coarse_inverse.shape
        lanes = 128 * pl.cdiv(primals, 128)
        anywhere = pl.BlockSpec(memory_space=pltpu.HBM)
        near = pl.BlockSpec(memory_space=pltpu.VMEM)
        fixed = 4 * size * size + 8 * face * face + 22 * size * cases
        slots = count * (4 * 8 * lanes + 8 * primals * width + 4 * primals * cases + 4 * 8 * cases)
        blocks = 4 * cols * width * cases
        limit = min(fixed + slots + blocks + 4 * 1024 * 1024, 63 * 1024 * 1024)
        first, alpha = pl.pallas_call(
            functools.partial(kernel, subs, cols),
            out_shape=(
                jax.ShapeDtypeStruct((size, cases), F32),
                jax.ShapeDtypeStruct((1, cases), F32),
            ),
            in_specs=[anywhere] * 7,
            out_specs=(near, near),
            scratch_shapes=[
                pltpu.VMEM(basis.shape, BF16),
                pltpu.VMEM(coarse_inverse.shape, BF16),
                pltpu.VMEM(primal_index.shape, jnp.int32),
                pltpu.VMEM(neighbour_dof.shape, jnp.int32),
                pltpu.VMEM((size, cases), BF16),
                pltpu.VMEM((size, size), BF16),
                pltpu.VMEM((size, size), BF16),
                pltpu.VMEM((4, face, face), BF16),
                pltpu.VMEM((4, face, cases), BF16),
                pltpu.VMEM((4, face, cases), BF16),
                pltpu.VMEM((size, cases), BF16),
                pltpu.VMEM((size, cases), F32),
                pltpu.VMEM((size, cases), BF16),
                pltpu.VMEM((size, cases), BF16),
                pltpu.VMEM((size, cases), F32),
                pltpu.VMEM((count, 1, lanes), F32),
                pltpu.VMEM((count, primals, width), BF16),
                pltpu.VMEM((count, primals, width), BF16),
                pltpu.VMEM((cols, width, cases), F32),
                pltpu.VMEM((count, primals, cases), BF16),
                pltpu.VMEM((count, 2, cases), F32),
                pltpu.SemaphoreType.DMA((8,)),
                pltpu.SemaphoreType.DMA((4,)),
                pltpu.SemaphoreType.DMA((4,)),
                pltpu.SemaphoreType.DMA((4,)),
                pltpu.SemaphoreType.DMA((4,)),
                pltpu.SemaphoreType.DMA((4,)),
                pltpu.SemaphoreType.DMA((4,)),
            ],
            compiler_params=pltpu.CompilerParams(
                collective_id=0, has_side_effects=True, vmem_limit_bytes=limit
            ),
        )(*(pltpu.with_memory_space_constraint(x, pltpu.HBM) for x in (rhs, schur, local_inverse, basis, coarse_inverse, primal_index, neighbour_dof)))
        return (alpha * first).astype(BF16)[None]

    return jax.shard_map(
        step,
        mesh=mesh,
        in_specs=(
            P(("sub", "col"), None, None),
            P(("sub", "col"), None, None),
            P(("sub", "col"), None, None),
            P(("sub", "col"), None, None),
            P("sub", "col"),
            P(("sub", "col"), None),
            P(("sub", "col"), None),
        ),
        out_specs=P(("sub", "col"), None, None),
        check_vma=False,
    )
```

```python
import functools
import math

import jax
import jax.numpy as jnp
from jax import lax
from jax.experimental import pallas as pl
from jax.experimental.pallas import tpu as pltpu
from jax.sharding import PartitionSpec as P

MESH = pl.DeviceIdType.MESH
F32 = jnp.float32
BF16 = jnp.bfloat16
UNROLL = True


def kernel(
    subs, cols,
    rhs_hbm, schur_hbm, inverse_hbm, basis_hbm, coarse_hbm, index_hbm, links_hbm,
    first_ref, alpha_ref,
    basis_ref, coarse_ref, index_ref, links_ref,
    rhs_ref, schur_ref, inverse_ref, picks, halo_rhs, halo_z, weighted, z_ref, z_half, p_half,
    image_ref, indices, chosen, arrived, columns, rows_ref, loads, sums,
    local_sem, halo_send, halo_recv, z_send, z_recv, all_send, all_recv,
):
    count = subs * cols
    row = lax.axis_index("sub")
    column = lax.axis_index("col")
    me = row * cols + column
    size = rhs_ref.shape[0]
    face = size // 4
    primals = index_ref.shape[1]
    height, width = coarse_ref.shape
    group = math.gcd(count, 32)

    def place(target):
        return (target // cols, target % cols)

    half_way = (row * 2) // subs

    def each_other(act):
        def body(step, carry):
            q = step // cols
            target_row = (1 - half_way) * (subs - 1 - q) + half_way * q
            target = target_row * cols + (column + step) % cols

            @pl.when(target != me)
            def _():
                act(target)

            return carry

        lax.fori_loop(0, count, body, 0, unroll=UNROLL and count <= 64)

    barrier = pltpu.get_barrier_semaphore()

    each_other(
        lambda target: pl.semaphore_signal(
            barrier, inc=1, device_id=place(target), device_id_type=MESH
        )
    )

    small_loads = [
        pltpu.make_async_copy(source, target, local_sem.at[4 + number])
        for number, (source, target) in enumerate(
            ((links_hbm, links_ref), (index_hbm, index_ref), (basis_hbm, basis_ref), (coarse_hbm, coarse_ref))
        )
    ]
    for load in small_loads:
        load.start()
    load_rhs = pltpu.make_async_copy(rhs_hbm.at[0], rhs_ref, local_sem.at[0])
    load_inverse = pltpu.make_async_copy(inverse_hbm.at[0], inverse_ref, local_sem.at[1])
    load_schur = pltpu.make_async_copy(schur_hbm.at[0], schur_ref, local_sem.at[2])
    load_rhs.start()
    load_inverse.start()
    load_schur.start()
    for load in small_loads:
        load.wait()

    lanes = indices.shape[2]
    indices[me] = jnp.zeros((1, lanes), F32)
    indices[me, :, pl.ds(0, primals)] = index_ref[...].astype(F32)

    offsets = (face, 0, 3 * face, 2 * face)
    for f in range(4):
        places = links_ref[:, f * face : (f + 1) * face] - offsets[f]
        hit = lax.broadcasted_iota(jnp.int32, (face, face), 0) == places
        picks[f] = jnp.where(hit, 1.0, 0.0).astype(F32).T.astype(BF16)

    pl.semaphore_wait(barrier, count - 1)

    swap = row % 2

    def halo_copies(source, target, send, recv):
        copies = []
        for g in (swap, 1 - swap, 2, 3):
            if isinstance(g, int):
                facing = 5 - g
                partner = (row, (column + cols + 2 * g - 5) % cols)
            else:
                facing = 1 - g
                partner = ((row + subs + 2 * g - 1) % subs, column)
            copies.append(
                pltpu.make_async_remote_copy(
                    src_ref=source(g),
                    dst_ref=target.at[facing],
                    send_sem=send.at[g],
                    recv_sem=recv.at[facing],
                    device_id=partner,
                    device_id_type=MESH,
                )
            )
        return copies

    def wait_face(target, recv, f):
        pltpu.make_async_copy(target.at[f], target.at[f], recv.at[f]).wait()

    def broadcast(slots, number):
        each_other(
            lambda target: pltpu.make_async_remote_copy(
                src_ref=slots.at[me],
                dst_ref=slots.at[me],
                send_sem=all_send.at[number],
                recv_sem=all_recv.at[number],
                device_id=place(target),
                device_id_type=MESH,
            ).start()
        )

    def wait_all(slots, sems, number):
        part = slots.at[pl.ds(0, count - 1)]
        pltpu.make_async_copy(part, part, sems.at[number]).wait()

    rhs_copies = halo_copies(
        lambda g: rhs_hbm.at[0, pl.ds(g * face, face)], halo_rhs, halo_send, halo_recv
    )
    broadcast(indices, 0)
    for copy in rhs_copies:
        copy.start()

    basis = basis_ref[0]
    basis_t = basis.astype(F32).T.astype(BF16)
    load_rhs.wait()

    wait_all(indices, all_recv, 0)

    def spread(g, extent):
        values = indices[pl.ds(g * group, group)]
        values = jnp.broadcast_to(values, (group, primals, lanes))
        diagonal = lax.broadcasted_iota(jnp.int32, values.shape, 1) == lax.broadcasted_iota(
            jnp.int32, values.shape, 2
        )
        named = jnp.sum(jnp.where(diagonal, values, 0.0), axis=2, keepdims=True)
        named = named.astype(jnp.int32)
        return jnp.broadcast_to(named, (group, primals, extent))

    def choose(g, carry):
        named = spread(g, height) - row * height
        hit = lax.broadcasted_iota(jnp.int32, named.shape, 2) == named
        hit = jnp.where(hit, 1.0, 0.0).astype(F32).reshape(group * primals, height).astype(BF16)
        picked = jnp.dot(hit, coarse_ref[...], preferred_element_type=F32)
        chosen[pl.ds(g * group, group)] = picked.reshape(group, primals, width).astype(BF16)
        return carry

    lax.fori_loop(0, count // group, choose, 0)
    arrived[me] = chosen[me]

    each_other(
        lambda target: pltpu.make_async_remote_copy(
            src_ref=chosen.at[target],
            dst_ref=arrived.at[me],
            send_sem=all_send.at[2],
            recv_sem=all_recv.at[2],
            device_id=place(target),
            device_id_type=MESH,
        ).start()
    )

    load = jnp.zeros((primals, rhs_ref.shape[1]), F32)
    for f in (2, 3, 0, 1):
        block = pl.ds(f * face, face)
        wait_face(halo_rhs, halo_recv, f)
        got = jnp.dot(picks[f], halo_rhs[f], preferred_element_type=F32)
        residual = rhs_ref[block, :].astype(F32) + got
        first_ref[block, :] = residual
        part = (residual * 0.5).astype(BF16)
        weighted[block, :] = part
        load += jnp.dot(basis[:, f * face : (f + 1) * face], part, preferred_element_type=F32)
    loads[me] = load.astype(BF16)
    broadcast(loads, 1)

    load_inverse.wait()
    for f in range(4):
        block = pl.ds(f * face, face)
        z_ref[block, :] = jnp.dot(inverse_ref[block, :], weighted[...], preferred_element_type=F32)

    wait_all(arrived, all_recv, 2)
    for j in range(cols):
        def add(i, total):
            return total + arrived[i * cols + j].astype(F32)

        rows_ref[j] = lax.fori_loop(0, subs, add, jnp.zeros((primals, width), F32), unroll=subs <= 8)

    def arrange(g, carry):
        total = jnp.zeros((primals, group * primals), F32)
        for j in range(cols):
            named = spread(g, width) - j * width
            hit = lax.broadcasted_iota(jnp.int32, named.shape, 2) == named
            hit = jnp.where(hit, 1.0, 0.0).astype(F32).reshape(group * primals, width).astype(BF16)
            total += lax.dot_general(
                rows_ref[j].astype(BF16), hit, (((1,), (1,)), ((), ())), preferred_element_type=F32
            )
        columns[g] = total
        return carry

    lax.fori_loop(0, count // group, arrange, 0)

    wait_all(loads, all_recv, 1)

    def solve(g, total):
        part = loads[pl.ds(g * group, group)].astype(F32).reshape(group * primals, loads.shape[2])
        return total + jnp.dot(columns[g].astype(BF16), part.astype(BF16), preferred_element_type=F32)

    taken = lax.fori_loop(
        0, count // group, solve, jnp.zeros((primals, loads.shape[2]), F32)
    ).astype(BF16)

    z_copies = halo_copies(lambda g: z_half.at[pl.ds(g * face, face)], halo_z, z_send, z_recv)
    for f in range(4):
        block = pl.ds(f * face, face)
        correction = jnp.dot(
            basis_t[f * face : (f + 1) * face, :], taken, preferred_element_type=F32
        )
        z_value = (z_ref[block, :] + correction) * 0.5
        z_ref[block, :] = z_value
        z_half[block, :] = z_value.astype(BF16)
        if f == 1:
            z_copies[0].start()
            z_copies[1].start()
        if f > 1:
            z_copies[f].start()
    sums[me, pl.ds(0, 1), :] = jnp.sum(first_ref[...] * z_ref[...], axis=0, keepdims=True)
    load_schur.wait()
    for pair in ((2, 3), (0, 1)):
        for f in pair:
            block = pl.ds(f * face, face)
            wait_face(halo_z, z_recv, f)
            first = z_ref[block, :] + jnp.dot(picks[f], halo_z[f], preferred_element_type=F32)
            first_ref[block, :] = first
            p_half[block, :] = first.astype(BF16)
        both = pl.ds(pair[0] * face, 2 * face)
        if pair[0] == 2:
            for f in range(4):
                block = pl.ds(f * face, face)
                image_ref[block, :] = jnp.dot(
                    schur_ref[block, both], p_half[both, :], preferred_element_type=F32
                )
    total = jnp.zeros((1, first_ref.shape[1]), F32)
    for f in range(4):
        block = pl.ds(f * face, face)
        image = image_ref[block, :] + jnp.dot(
            schur_ref[block, both], p_half[both, :], preferred_element_type=F32
        )
        total += jnp.sum(first_ref[block, :] * image, axis=0, keepdims=True)
    sums[me, pl.ds(1, 1), :] = total
    broadcast(sums, 3)
    for copy in rhs_copies + z_copies:
        copy.wait_send()
    wait_all(indices, all_send, 0)
    wait_all(loads, all_send, 1)
    wait_all(arrived, all_send, 2)
    wait_all(sums, all_recv, 3)
    whole = jnp.sum(sums[...], axis=0)
    alpha_ref[...] = whole[0:1, :] / whole[1:2, :]
    wait_all(sums, all_send, 3)


def solution(mesh):
    subs, cols = mesh.shape["sub"], mesh.shape["col"]
    count = subs * cols

    def step(rhs, schur, local_inverse, basis, coarse_inverse, primal_index, neighbour_dof):
        size, cases = rhs.shape[1:]
        face = size // 4
        primals = primal_index.shape[1]
        height, width = coarse_inverse.shape
        lanes = 128 * pl.cdiv(primals, 128)
        anywhere = pl.BlockSpec(memory_space=pltpu.HBM)
        near = pl.BlockSpec(memory_space=pltpu.VMEM)
        fixed = 4 * size * size + 8 * face * face + 22 * size * cases
        slots = count * (4 * 8 * lanes + 8 * primals * width + 4 * primals * cases + 4 * 8 * cases)
        blocks = 4 * primals * (count * primals + cols * width)
        group = math.gcd(count, 32)
        limit = min(fixed + slots + blocks + 4 * 1024 * 1024, 63 * 1024 * 1024)
        first, alpha = pl.pallas_call(
            functools.partial(kernel, subs, cols),
            out_shape=(
                jax.ShapeDtypeStruct((size, cases), F32),
                jax.ShapeDtypeStruct((1, cases), F32),
            ),
            in_specs=[anywhere] * 7,
            out_specs=(near, near),
            scratch_shapes=[
                pltpu.VMEM(basis.shape, BF16),
                pltpu.VMEM(coarse_inverse.shape, BF16),
                pltpu.VMEM(primal_index.shape, jnp.int32),
                pltpu.VMEM(neighbour_dof.shape, jnp.int32),
                pltpu.VMEM((size, cases), BF16),
                pltpu.VMEM((size, size), BF16),
                pltpu.VMEM((size, size), BF16),
                pltpu.VMEM((4, face, face), BF16),
                pltpu.VMEM((4, face, cases), BF16),
                pltpu.VMEM((4, face, cases), BF16),
                pltpu.VMEM((size, cases), BF16),
                pltpu.VMEM((size, cases), F32),
                pltpu.VMEM((size, cases), BF16),
                pltpu.VMEM((size, cases), BF16),
                pltpu.VMEM((size, cases), F32),
                pltpu.VMEM((count, 1, lanes), F32),
                pltpu.VMEM((count, primals, width), BF16),
                pltpu.VMEM((count, primals, width), BF16),
                pltpu.VMEM((count // group, primals, group * primals), F32),
                pltpu.VMEM((cols, primals, width), F32),
                pltpu.VMEM((count, primals, cases), BF16),
                pltpu.VMEM((count, 2, cases), F32),
                pltpu.SemaphoreType.DMA((8,)),
                pltpu.SemaphoreType.DMA((4,)),
                pltpu.SemaphoreType.DMA((4,)),
                pltpu.SemaphoreType.DMA((4,)),
                pltpu.SemaphoreType.DMA((4,)),
                pltpu.SemaphoreType.DMA((4,)),
                pltpu.SemaphoreType.DMA((4,)),
            ],
            compiler_params=pltpu.CompilerParams(
                collective_id=0, has_side_effects=True, vmem_limit_bytes=limit
            ),
        )(*(pltpu.with_memory_space_constraint(x, pltpu.HBM) for x in (rhs, schur, local_inverse, basis, coarse_inverse, primal_index, neighbour_dof)))
        return (alpha * first).astype(BF16)[None]

    return jax.shard_map(
        step,
        mesh=mesh,
        in_specs=(
            P(("sub", "col"), None, None),
            P(("sub", "col"), None, None),
            P(("sub", "col"), None, None),
            P(("sub", "col"), None, None),
            P("sub", "col"),
            P(("sub", "col"), None),
            P(("sub", "col"), None),
        ),
        out_specs=P(("sub", "col"), None, None),
        check_vma=False,
    )
```
